512 devices in a mesh: dom: 32 (over x, z), wide: 16 (over y, core).
Axes of the slice: x: 4, y: 8, z: 8, core: 2. Of those that a mesh axis runs over, the one named last changes fastest.
Arguments:
- features: bfloat16 [131072, 512], P(('dom', 'wide')), may hold values from -6 to 6
- w_self: bfloat16 [512, 512], replicated, may hold values from -0.25 to 0.25
- w_neigh: bfloat16 [512, 512], replicated, may hold values from -0.25 to 0.25
- boundary: int32 [512, 2, 64], P(('dom', 'wide')), may hold values from 0 to 255
- neighbors: int32 [131072, 16], P(('dom', 'wide')), may hold values from 0 to 384, as said below
- anchors: int32 [8192, 32], P(('dom', 'wide')), may hold values from 0 to 255
- negatives: int32 [8192, 32, 8], P(('dom', 'wide')), may hold values from 0 to 255
- positives: int32 [131072, 2], P(('dom', 'wide')), may hold values from 0 to 255
Outputs:
- embed: bfloat16 [131072, 512], P(('dom', 'wide'))
- embed_grad: bfloat16 [131072, 512], P(('dom', 'wide'))
The draws below stay inside these ranges and needn't reach their ends.
Inputs may be any that keep to these rules, and one draw needn't show every extreme that they name: `neighbors`: each row has its live slots first, 1 to 16 of them; the first node of every partition has 16; slots after the live ones hold 384. `anchors`: rows of the own partition. `negatives`: rows of the own partition. `positives`: rows of the own partition.
All inputs are finite; a program needn't handle non-finite values.
Results may differ from the reference program's by a relative error of at most 0.0053.
Values may be sent and summed in bfloat16 or wider, within the bound.
No kernel may reach another device: no remote copies, remote signals or barrier semaphores. Data moves between devices by JAX's collectives and lax.ppermute only.
A program may use at most 64 MiB of HBM per device.

```python
import math
import jax
import jax.numpy as jnp
from jax import lax

D = 512
NODE_DEV = 256
DEG = 16
ANCH = 32
K = 8
BND = 64
TABLE = 384
NODES = 131072
N_DOM = 32
N_WIDE = 16


def draw_neighbors(key, part):
    key_deg, key_idx = jax.random.split(jax.random.fold_in(key, 11))
    degree = jax.random.randint(key_deg, (NODES, 1), 1, DEG + 1)
    rows = jnp.arange(NODES)[:, None]
    degree = jnp.where(rows % NODE_DEV == 0, DEG, degree)
    index = jax.random.randint(key_idx, (NODES, DEG), 0, TABLE)
    slots = jnp.arange(DEG)[None, :]
    return jnp.where(slots < degree, index, TABLE).astype(jnp.int32)


def place_ends(values, key, low, largest):
    index_at = [jax.random.randint(jax.random.fold_in(key, axis), (), 0, length) for axis, length in enumerate(values.shape)]
    longest = values.shape.index(max(values.shape))
    neighbour = index_at[:longest] + [(index_at[longest] + 1) % values.shape[longest]] + index_at[longest + 1:]
    return values.at[tuple(index_at)].set(low).at[tuple(neighbour)].set(largest)


def block_levels(key, shape, cuts, least, high):
    gain = 1.0
    for position, shards_of in cuts:
        steps = jax.random.uniform(jax.random.fold_in(jax.random.fold_in(key, 6), position), (shards_of,), jnp.float32, least / len(cuts), high / len(cuts))
        gain = gain * jnp.repeat(jnp.exp(steps), shape[position] // shards_of).reshape((-1,) + (1,) * (len(shape) - 1 - position))
    return gain


def normal_values(stream_key, extent, deviation, bound, pieces=(), kind=jnp.bfloat16):
    result = deviation * jax.random.normal(stream_key, extent, jnp.float32)
    if pieces:
        result = result * block_levels(stream_key, extent, pieces, -0.22, 0.18)
    return jnp.clip(result, -bound, bound).astype(kind)


def setup_inputs(seed: int = 0) -> dict:
    key_of = jax.random.split(jax.random.key(seed), 9)
    features = normal_values(key_of[0], (NODES, D), 1.0, 6.0, ((0, 512),))
    w_self = normal_values(key_of[1], (D, D), D ** -0.5, 0.25)
    w_neigh = normal_values(key_of[2], (D, D), D ** -0.5, 0.25)
    boundary = place_ends(jax.random.randint(key_of[3], (N_DOM * N_WIDE, 2, BND), 0, NODE_DEV), jax.random.fold_in(key_of[3], 1), 0, NODE_DEV - 1).astype(jnp.int32)
    neighbors = draw_neighbors(jax.random.fold_in(key_of[8], 71), 0)
    anchors = place_ends(jax.random.randint(key_of[5], (N_DOM * N_WIDE * N_WIDE, ANCH), 0, NODE_DEV), jax.random.fold_in(key_of[5], 1), 0, NODE_DEV - 1).astype(jnp.int32)
    negatives = place_ends(jax.random.randint(key_of[6], (N_DOM * N_WIDE * N_WIDE, ANCH, K), 0, NODE_DEV), jax.random.fold_in(key_of[6], 1), 0, NODE_DEV - 1).astype(jnp.int32)
    positives = place_ends(jax.random.randint(key_of[7], (NODES, 2), 0, NODE_DEV), jax.random.fold_in(key_of[7], 1), 0, NODE_DEV - 1).astype(jnp.int32)
    return {"features": features, "w_self": w_self, "w_neigh": w_neigh, "boundary": boundary, "neighbors": neighbors, "anchors": anchors, "negatives": negatives, "positives": positives}


def reference(features, w_self, w_neigh, boundary, neighbors, anchors, negatives, positives):
    scale = 1.0 / math.sqrt(D)
    parts = N_DOM * N_WIDE
    xs = features.reshape(N_DOM, N_WIDE, NODE_DEV, D)
    bnd = boundary.reshape(N_DOM, N_WIDE, 2, BND)
    take = jax.vmap(jax.vmap(lambda x, i: x[i]))
    upward = take(xs, bnd[:, :, 0])
    downward = take(xs, bnd[:, :, 1])
    zero_rows = jnp.zeros_like(upward[:1])
    below = jnp.concatenate([zero_rows, upward[:-1]], axis=0)
    above = jnp.concatenate([downward[1:], zero_rows], axis=0)
    pad_row = jnp.zeros((N_DOM, N_WIDE, 1, D), jnp.bfloat16)
    tables = jnp.concatenate([xs, below, above, pad_row], axis=2).reshape(parts, TABLE + 1, D)
    nbrs = neighbors.reshape(parts, NODE_DEV, DEG)
    feats = features.reshape(parts, NODE_DEV, D)

    def layer(args):
        table, nbr, own = args
        summed = lax.optimization_barrier(jnp.sum(table[nbr].astype(jnp.float32), axis=1))
        degree = lax.optimization_barrier(jnp.sum((nbr < TABLE).astype(jnp.float32), axis=1))
        mean = (summed / degree[:, None]).astype(jnp.bfloat16)
        out = jnp.dot(own, w_self, preferred_element_type=jnp.float32) + jnp.dot(mean, w_neigh, preferred_element_type=jnp.float32)
        return out.astype(jnp.bfloat16)
    embed = lax.map(layer, (tables, nbrs, feats))
    hs = embed.reshape(N_DOM, N_WIDE, NODE_DEV, D)
    anc = anchors.reshape(N_DOM, N_WIDE, N_WIDE, ANCH)
    neg = negatives.reshape(N_DOM, N_WIDE, N_WIDE, ANCH, K)
    pos = positives.reshape(N_DOM, N_WIDE, NODE_DEV, 2)
    pick = jax.vmap(lambda g, i: g[i])

    def per_part(t):
        dom_i = t // N_WIDE
        wide_i = t % N_WIDE
        group = hs[dom_i]
        mine = group[wide_i]
        group_anc = anc[dom_i]
        group_neg = neg[dom_i]
        a_rows = mine[group_anc[wide_i]].astype(jnp.float32)
        r_rows = pick(group, group_neg[:, wide_i]).astype(jnp.float32)
        coef = jax.nn.sigmoid(jnp.einsum('jad,jakd->jak', a_rows, r_rows) * scale)
        anchor_terms = jnp.einsum('jak,jakd->jad', coef, r_rows)
        grad = jax.ops.segment_sum(anchor_terms.reshape(-1, D), group_anc[wide_i].reshape(-1), NODE_DEV)
        s_rows = pick(group, group_anc[:, wide_i]).astype(jnp.float32)
        o_rows = mine[group_neg[wide_i]].astype(jnp.float32)
        coef2 = jax.nn.sigmoid(jnp.einsum('vad,vakd->vak', s_rows, o_rows) * scale)
        owner_terms = coef2[..., None] * s_rows[:, :, None, :]
        grad = grad + jax.ops.segment_sum(owner_terms.reshape(-1, D), group_neg[wide_i].reshape(-1), NODE_DEV)
        pairs = pos[dom_i, wide_i]
        hu = mine[pairs[:, 0]].astype(jnp.float32)
        hv = mine[pairs[:, 1]].astype(jnp.float32)
        coef3 = jax.nn.sigmoid(lax.optimization_barrier(jnp.sum(hu * hv, axis=1)) * scale) - 1.0
        grad = grad + jax.ops.segment_sum(coef3[:, None] * hv, pairs[:, 0], NODE_DEV)
        grad = grad + jax.ops.segment_sum(coef3[:, None] * hu, pairs[:, 1], NODE_DEV)
        return grad.astype(jnp.bfloat16)
    grads = lax.map(per_part, jnp.arange(parts, dtype=jnp.int32))
    return (embed.reshape(NODES, D), grads.reshape(NODES, D))
```

```python
import functools
import math

import jax
import jax.numpy as jnp
from jax import lax
from jax.experimental import pallas as pl
from jax.experimental.pallas import tpu as pltpu
from jax.sharding import PartitionSpec as P

F32 = jnp.float32
BF16 = jnp.bfloat16


def shape(dims, dtype):
    return pltpu.VMEM(dims, dtype)


def call(kernel, outs, *operands, from_hbm=0, **static):
    spaces = [pltpu.HBM] * from_hbm + [pltpu.VMEM] * (len(operands) - from_hbm)
    return pl.pallas_call(
        functools.partial(kernel, **static) if static else kernel,
        out_shape=outs,
        in_specs=[pl.BlockSpec(memory_space=space) for space in spaces],
        out_specs=[pl.BlockSpec(memory_space=pltpu.VMEM)] * len(outs),
        scratch_shapes=[pltpu.SemaphoreType.DMA((from_hbm,))] if from_hbm else [],
        compiler_params=pltpu.CompilerParams(vmem_limit_bytes=4 * 2**20),
        name=kernel.__name__,
    )(*[pltpu.with_memory_space_constraint(x, space) for x, space in zip(operands, spaces)])


def fetch(pairs, arrived):
    copies = [pltpu.make_async_copy(a, b, arrived.at[n]) for n, (a, b) in enumerate(pairs)]
    for copy in copies:
        copy.start()
    return copies


def dot(a, b):
    return jnp.dot(a, b, preferred_element_type=F32)


def dot_nt(a, b):
    return lax.dot_general(a, b, (((1,), (1,)), ((), ())), preferred_element_type=F32)


def dot_tn(a, b):
    return lax.dot_general(a, b, (((0,), (0,)), ((), ())), preferred_element_type=F32)


def column_counts(columns, width, offset=0):
    rows, slots = columns.shape
    lanes = lax.broadcasted_iota(jnp.int32, (rows, width), 1) + offset
    total = jnp.zeros((rows, width), F32)
    for slot in range(slots):
        total = total + jnp.where(columns[:, slot : slot + 1] == lanes, 1.0, 0.0)
    return total


def row_counts(rows, height):
    slots, width = rows.shape
    levels = lax.broadcasted_iota(jnp.int32, (height, width), 0)
    total = jnp.zeros((height, width), F32)
    for slot in range(slots):
        total = total + jnp.where(rows[slot : slot + 1, :] == levels, 1.0, 0.0)
    return total


def head_kernel(*refs):
    fetched = 4
    held, (up_ref, down_ref, arrived) = refs[fetched : 2 * fetched], refs[2 * fetched :]
    copies = fetch(zip(refs[:fetched], held), arrived)
    lists_ref, features_ref = held[:2]
    copies[0].wait()
    nodes = features_ref.shape[0]
    onehots = [row_counts(lists_ref[0, side : side + 1, :], nodes).astype(BF16) for side in range(2)]
    copies[1].wait()
    for onehot, out in zip(onehots, (up_ref, down_ref)):
        out[...] = dot_tn(onehot, features_ref[...]).astype(BF16)
    for copy in copies[2:]:
        copy.wait()


def own_kernel(*refs):
    fetched = 4
    given, (features_ref, neighbors_ref, anchors_ref) = refs[:fetched], refs[fetched : fetched + 3]
    held = refs[fetched + 3 : 2 * fetched + 3]
    own_ref, summed_ref, counts_ref, degree_ref, pick_ref, arrived = refs[2 * fetched + 3 :]
    copies = fetch(zip(given, held), arrived)
    features = features_ref[...]
    nodes = features.shape[0]
    edge = counts_ref.shape[1]
    counts = column_counts(neighbors_ref[...].T, nodes + edge)
    degree_ref[...] = jnp.sum(counts, axis=1, keepdims=True)
    counts = counts.astype(BF16)
    counts_ref[...] = counts[:, nodes:]
    summed_ref[...] = dot(counts[:, :nodes], features)
    slots = jnp.concatenate([anchors_ref[j : j + 1, :] for j in range(anchors_ref.shape[0])], axis=1)
    pick_ref[...] = column_counts(slots.T, nodes).astype(BF16)
    copies[0].wait()
    own_ref[...] = dot(features, held[0][...])
    for copy in copies[1:]:
        copy.wait()


def embed_kernel(below_ref, above_ref, counts_ref, degree_ref, summed_ref, own_ref, w_neigh_ref, pick_ref, embed_ref, rows_ref):
    rows = below_ref.shape[0]
    summed = summed_ref[...] + dot(counts_ref[:, :rows], below_ref[...]) + dot(counts_ref[:, rows:], above_ref[...])
    mean = (summed / degree_ref[...]).astype(BF16)
    embed = (own_ref[...] + dot(mean, w_neigh_ref[...])).astype(BF16)
    embed_ref[...] = embed
    rows_ref[...] = dot(pick_ref[...], embed).astype(BF16)


def local_kernel(negatives_ref, positives_ref, anchors_ref, embed_ref, live_ref, spread_ref, grad_ref, *, scale):
    embed = embed_ref[...]
    nodes = embed.shape[0]
    peers = negatives_ref.shape[0]
    slots = jnp.concatenate([negatives_ref[j] for j in range(peers)], axis=1)
    live_ref[...] = column_counts(slots.T, nodes).astype(BF16)
    anchors = jnp.concatenate([anchors_ref[j : j + 1, :] for j in range(peers)], axis=1)
    spread_ref[...] = row_counts(anchors, nodes).astype(BF16)
    first = row_counts(positives_ref[0:1, :], nodes).astype(BF16)
    second = row_counts(positives_ref[1:2, :], nodes).astype(BF16)
    pairs = dot_nt(first, second) + dot_nt(second, first)
    weight = (jax.nn.sigmoid(dot_nt(embed, embed) * scale) - 1.0) * pairs
    grad_ref[...] = dot(weight.astype(BF16), embed)


def score_kernel(got_ref, embed_ref, live_ref, weight_ref, back_ref, *, scale):
    embed = embed_ref[...]
    weight = jax.nn.sigmoid(dot_nt(got_ref[...], embed) * scale) * live_ref[...].astype(F32)
    weight = weight.astype(BF16)
    weight_ref[...] = weight
    back_ref[...] = dot(weight, embed).astype(BF16)


def owner_kernel(weight_ref, got_ref, grad_ref, out_ref):
    out_ref[...] = grad_ref[...] + dot_tn(weight_ref[...], got_ref[...])


def final_kernel(spread_ref, terms_ref, grad_ref, out_ref):
    out_ref[...] = (grad_ref[...] + dot(spread_ref[...], terms_ref[...])).astype(BF16)


def passed_along(block, axis, distance):
    devices = range(lax.axis_size(axis))
    route = [(i - distance, i) for i in devices if i - distance in devices]
    return lax.ppermute(block, axis, route)


def exchanged(rows, peers):
    block = rows.reshape(peers, -1, rows.shape[1])
    return lax.all_to_all(block, "wide", split_axis=0, concat_axis=0, tiled=True).reshape(rows.shape)


def body(features, w_self, w_neigh, boundary, neighbors, anchors, negatives, positives):
    nodes, width = features.shape
    scale = 1.0 / math.sqrt(width)
    peers, anch = anchors.shape
    slots = peers * anch
    edge = boundary.shape[2]
    given = (boundary, features, neighbors.T, anchors)
    _, features, neighbors, anchors, up, down = call(
        head_kernel,
        [shape(x.shape, x.dtype) for x in given] + [shape((edge, width), BF16)] * 2,
        *given,
        from_hbm=len(given),
    )
    below = passed_along(up, "dom", 1)
    above = passed_along(down, "dom", -1)
    given = (w_self, w_neigh, negatives.transpose(0, 2, 1), positives.T)
    _, w_neigh, negatives, positives, own, summed, counts, degree, pick = call(
        own_kernel,
        [shape(x.shape, x.dtype) for x in given]
        + [
            shape((nodes, width), F32),
            shape((nodes, width), F32),
            shape((nodes, 2 * edge), BF16),
            shape((nodes, 1), F32),
            shape((slots, nodes), BF16),
        ],
        *given,
        features,
        neighbors,
        anchors,
        from_hbm=len(given),
    )
    embed, rows = call(
        embed_kernel,
        [shape((nodes, width), BF16), shape((slots, width), BF16)],
        below,
        above,
        counts,
        degree,
        summed,
        own,
        w_neigh,
        pick,
    )
    got = exchanged(rows, peers)
    live, spread, grad = call(
        local_kernel,
        [shape((slots, nodes), BF16), shape((nodes, slots), BF16), shape((nodes, width), F32)],
        negatives,
        positives,
        anchors,
        embed,
        scale=scale,
    )
    weight, back = call(
        score_kernel,
        [shape((slots, nodes), BF16), shape((slots, width), BF16)],
        got,
        embed,
        live,
        scale=scale,
    )
    terms = exchanged(back, peers)
    [grad] = call(owner_kernel, [shape((nodes, width), F32)], weight, got, grad)
    [out] = call(final_kernel, [shape((nodes, width), BF16)], spread, terms, grad)
    return (embed, out)


def solution(mesh):
    split = P(("dom", "wide"))
    return jax.shard_map(
        body,
        mesh=mesh,
        in_specs=(split, P(), P(), split, split, split, split, split),
        out_specs=(split, split),
        check_vma=False,
    )
```

```python
import functools
import math

import jax
import jax.numpy as jnp
from jax import lax
from jax.experimental import pallas as pl
from jax.experimental.pallas import tpu as pltpu
from jax.sharding import PartitionSpec as P

F32 = jnp.float32
BF16 = jnp.bfloat16


def shape(dims, dtype):
    return pltpu.VMEM(dims, dtype)


def call(kernel, outs, *operands, from_hbm=0, scratch=(), **static):
    spaces = [pltpu.HBM] * from_hbm + [pltpu.VMEM] * (len(operands) - from_hbm)
    return pl.pallas_call(
        functools.partial(kernel, **static) if static else kernel,
        out_shape=outs,
        in_specs=[pl.BlockSpec(memory_space=space) for space in spaces],
        out_specs=[pl.BlockSpec(memory_space=pltpu.VMEM)] * len(outs),
        scratch_shapes=list(scratch),
        compiler_params=pltpu.CompilerParams(vmem_limit_bytes=4 * 2**20),
        name=kernel.__name__,
    )(*[pltpu.with_memory_space_constraint(x, space) for x, space in zip(operands, spaces)])


def fetch(pairs, arrived):
    copies = [pltpu.make_async_copy(a, b, arrived.at[n]) for n, (a, b) in enumerate(pairs)]
    for copy in copies:
        copy.start()
    return copies


def dot(a, b):
    return jnp.dot(a, b, preferred_element_type=F32)


def dot_nt(a, b):
    return lax.dot_general(a, b, (((1,), (1,)), ((), ())), preferred_element_type=F32)


def dot_tn(a, b):
    return lax.dot_general(a, b, (((0,), (0,)), ((), ())), preferred_element_type=F32)


def column_counts(columns, width, offset=0):
    rows, slots = columns.shape
    lanes = lax.broadcasted_iota(jnp.int32, (rows, width), 1) + offset
    total = jnp.zeros((rows, width), F32)
    for slot in range(slots):
        total = total + jnp.where(columns[:, slot : slot + 1] == lanes, 1.0, 0.0)
    return total


def row_counts(rows, height):
    slots, width = rows.shape
    levels = lax.broadcasted_iota(jnp.int32, (height, width), 0)
    total = jnp.zeros((height, width), F32)
    for slot in range(slots):
        total = total + jnp.where(rows[slot : slot + 1, :] == levels, 1.0, 0.0)
    return total


def head_kernel(*refs):
    fetched = 5
    held, (pick_ref, up_ref, down_ref, arrived) = refs[fetched : 2 * fetched], refs[2 * fetched :]
    copies = fetch(zip(refs[:fetched], held), arrived)
    lists_ref, anchors_ref, features_ref = held[:3]
    nodes = features_ref.shape[0]
    copies[0].wait()
    onehots = [row_counts(lists_ref[0, side : side + 1, :], nodes).astype(BF16) for side in range(2)]
    copies[1].wait()
    slots = jnp.concatenate([anchors_ref[j : j + 1, :] for j in range(anchors_ref.shape[0])], axis=1)
    pick_ref[...] = column_counts(slots.T, nodes).astype(BF16)
    copies[2].wait()
    for onehot, out in zip(onehots, (up_ref, down_ref)):
        out[...] = dot_tn(onehot, features_ref[...]).astype(BF16)
    for copy in copies[3:]:
        copy.wait()


def own_kernel(features_ref, neighbors_ref, w_self_ref, own_ref, summed_ref, counts_ref, degree_ref):
    features = features_ref[...]
    nodes = features.shape[0]
    edge = counts_ref.shape[1]
    counts = column_counts(neighbors_ref[...].T, nodes + edge)
    degree_ref[...] = jnp.sum(counts, axis=1, keepdims=True)
    counts = counts.astype(BF16)
    counts_ref[...] = counts[:, nodes:]
    summed_ref[...] = dot(counts[:, :nodes], features)
    own_ref[...] = dot(features, w_self_ref[...])


def embed_kernel(below_ref, above_ref, counts_ref, degree_ref, summed_ref, own_ref, w_neigh_ref, pick_ref, embed_ref, rows_ref):
    rows = below_ref.shape[0]
    summed = summed_ref[...] + dot(counts_ref[:, :rows], below_ref[...]) + dot(counts_ref[:, rows:], above_ref[...])
    mean = (summed / degree_ref[...]).astype(BF16)
    embed = (own_ref[...] + dot(mean, w_neigh_ref[...])).astype(BF16)
    embed_ref[...] = embed
    rows_ref[...] = dot(pick_ref[...], embed).astype(BF16)


def local_kernel(negatives_ref, positives_ref, anchors_ref, embed_ref, live_ref, spread_ref, grad_ref, *, scale):
    embed = embed_ref[...]
    nodes = embed.shape[0]
    peers = negatives_ref.shape[0]
    slots = jnp.concatenate([negatives_ref[j] for j in range(peers)], axis=1)
    live_ref[...] = column_counts(slots.T, nodes).astype(BF16)
    anchors = jnp.concatenate([anchors_ref[j : j + 1, :] for j in range(peers)], axis=1)
    spread_ref[...] = row_counts(anchors, nodes).astype(BF16)
    first = row_counts(positives_ref[0:1, :], nodes).astype(BF16)
    second = row_counts(positives_ref[1:2, :], nodes).astype(BF16)
    pairs = dot_nt(first, second) + dot_nt(second, first)
    weight = (jax.nn.sigmoid(dot_nt(embed, embed) * scale) - 1.0) * pairs
    grad_ref[...] = dot(weight.astype(BF16), embed)


def score_kernel(got_ref, embed_ref, live_ref, weight_ref, back_ref, *, scale):
    embed = embed_ref[...]
    weight = jax.nn.sigmoid(dot_nt(got_ref[...], embed) * scale) * live_ref[...].astype(F32)
    weight = weight.astype(BF16)
    weight_ref[...] = weight
    back_ref[...] = dot(weight, embed).astype(BF16)


def owner_kernel(weight_ref, got_ref, grad_ref, out_ref):
    out_ref[...] = grad_ref[...] + dot_tn(weight_ref[...], got_ref[...])


def final_kernel(spread_ref, terms_ref, grad_ref, out_ref):
    out_ref[...] = (grad_ref[...] + dot(spread_ref[...], terms_ref[...])).astype(BF16)


def passed_along(block, axis, distance):
    devices = range(lax.axis_size(axis))
    route = [(i - distance, i) for i in devices if i - distance in devices]
    return lax.ppermute(block, axis, route)


def exchanged(rows, peers):
    block = rows.reshape(peers, -1, rows.shape[1])
    return lax.all_to_all(block, "wide", split_axis=0, concat_axis=0, tiled=True).reshape(rows.shape)


def body(features, w_self, w_neigh, boundary, neighbors, anchors, negatives, positives):
    nodes, width = features.shape
    scale = 1.0 / math.sqrt(width)
    peers, anch = anchors.shape
    slots = peers * anch
    edge = boundary.shape[2]
    given = (boundary, anchors, features, neighbors.T, w_self)
    _, anchors, features, neighbors, w_self, pick, up, down = call(
        head_kernel,
        [shape(x.shape, x.dtype) for x in given] + [shape((slots, nodes), BF16)] + [shape((edge, width), BF16)] * 2,
        *given,
        from_hbm=len(given),
        scratch=[pltpu.SemaphoreType.DMA((len(given),))],
    )
    below = passed_along(up, "dom", 1)
    above = passed_along(down, "dom", -1)
    own, summed, counts, degree = call(
        own_kernel,
        [
            shape((nodes, width), F32),
            shape((nodes, width), F32),
            shape((nodes, 2 * edge), BF16),
            shape((nodes, 1), F32),
        ],
        features,
        neighbors,
        w_self,
    )
    embed, rows = call(
        embed_kernel,
        [shape((nodes, width), BF16), shape((slots, width), BF16)],
        below,
        above,
        counts,
        degree,
        summed,
        own,
        w_neigh,
        pick,
    )
    got = exchanged(rows, peers)
    live, spread, grad = call(
        local_kernel,
        [shape((slots, nodes), BF16), shape((nodes, slots), BF16), shape((nodes, width), F32)],
        negatives.transpose(0, 2, 1),
        positives.T,
        anchors,
        embed,
        scale=scale,
    )
    weight, back = call(
        score_kernel,
        [shape((slots, nodes), BF16), shape((slots, width), BF16)],
        got,
        embed,
        live,
        scale=scale,
    )
    terms = exchanged(back, peers)
    [grad] = call(owner_kernel, [shape((nodes, width), F32)], weight, got, grad)
    [out] = call(final_kernel, [jax.ShapeDtypeStruct((nodes, width), BF16)], spread, terms, grad)
    return (embed, out)


def solution(mesh):
    split = P(("dom", "wide"))
    return jax.shard_map(
        body,
        mesh=mesh,
        in_specs=(split, P(), P(), split, split, split, split, split),
        out_specs=(split, split),
        check_vma=False,
    )
```

```python
import functools
import math

import jax
import jax.numpy as jnp
from jax import lax
from jax.experimental import pallas as pl
from jax.experimental.pallas import tpu as pltpu
from jax.sharding import PartitionSpec as P

F32 = jnp.float32
BF16 = jnp.bfloat16


def shape(dims, dtype):
    return pltpu.VMEM(dims, dtype)


def call(kernel, outs, *operands, from_hbm=0, scratch=(), **static):
    spaces = [pltpu.HBM] * from_hbm + [pltpu.VMEM] * (len(operands) - from_hbm)
    return pl.pallas_call(
        functools.partial(kernel, **static) if static else kernel,
        out_shape=outs,
        in_specs=[pl.BlockSpec(memory_space=space) for space in spaces],
        out_specs=[pl.BlockSpec(memory_space=pltpu.VMEM)] * len(outs),
        scratch_shapes=list(scratch),
        compiler_params=pltpu.CompilerParams(vmem_limit_bytes=4 * 2**20),
        name=kernel.__name__,
    )(*[pltpu.with_memory_space_constraint(x, space) for x, space in zip(operands, spaces)])


def fetch(pairs, arrived):
    copies = [pltpu.make_async_copy(a, b, arrived.at[n]) for n, (a, b) in enumerate(pairs)]
    for copy in copies:
        copy.start()
    return copies


def dot(a, b):
    return jnp.dot(a, b, preferred_element_type=F32)


def dot_nt(a, b):
    return lax.dot_general(a, b, (((1,), (1,)), ((), ())), preferred_element_type=F32)


def dot_tn(a, b):
    return lax.dot_general(a, b, (((0,), (0,)), ((), ())), preferred_element_type=F32)


def column_counts(columns, width):
    rows, slots = columns.shape
    lanes = (lax.broadcasted_iota(jnp.int32, (rows, width), 1) - 128).astype(BF16)
    columns = (columns - 128).astype(BF16)
    total = jnp.zeros((rows, width), BF16)
    one, zero = jnp.ones((), BF16), jnp.zeros((), BF16)
    for slot in range(slots):
        total = total + jnp.where(columns[:, slot : slot + 1] == lanes, one, zero)
    return total


def row_counts(rows, height):
    slots, width = rows.shape
    levels = lax.broadcasted_iota(jnp.int32, (height, width), 0)
    total = jnp.zeros((height, width), F32)
    for slot in range(slots):
        total = total + jnp.where(rows[slot : slot + 1, :] == levels, 1.0, 0.0)
    return total


def head_kernel(*refs):
    fetched = 4
    held, (pick_ref, up_ref, down_ref, arrived) = refs[fetched : 2 * fetched], refs[2 * fetched :]
    copies = fetch(zip(refs[:fetched], held), arrived)
    lists_ref, anchors_ref, features_ref = held[:3]
    nodes = features_ref.shape[0]
    copies[0].wait()
    onehots = [row_counts(lists_ref[0, side : side + 1, :], nodes).astype(BF16) for side in range(2)]
    copies[1].wait()
    slots = jnp.concatenate([anchors_ref[j : j + 1, :] for j in range(anchors_ref.shape[0])], axis=1)
    pick_ref[...] = column_counts(slots.T, nodes)
    copies[2].wait()
    for onehot, out in zip(onehots, (up_ref, down_ref)):
        out[...] = dot_tn(onehot, features_ref[...]).astype(BF16)
    for copy in copies[3:]:
        copy.wait()


def own_kernel(w_self_hbm, features_ref, neighbors_ref, own_ref, summed_ref, counts_ref, degree_ref, w_self_ref, arrived):
    [copy] = fetch(((w_self_hbm, w_self_ref),), arrived)
    features = features_ref[...]
    nodes = features.shape[0]
    edge = counts_ref.shape[1]
    counts = column_counts(neighbors_ref[...].T, nodes + edge)
    degree_ref[...] = jnp.sum(counts.astype(F32), axis=1, keepdims=True)
    counts_ref[...] = counts[:, nodes:]
    summed_ref[...] = dot(counts[:, :nodes], features)
    copy.wait()
    own_ref[...] = dot(features, w_self_ref[...])


def embed_kernel(below_ref, above_ref, counts_ref, degree_ref, summed_ref, own_ref, w_neigh_ref, pick_ref, embed_ref, rows_ref):
    rows = below_ref.shape[0]
    summed = summed_ref[...] + dot(counts_ref[:, :rows], below_ref[...]) + dot(counts_ref[:, rows:], above_ref[...])
    mean = (summed / degree_ref[...]).astype(BF16)
    embed = (own_ref[...] + dot(mean, w_neigh_ref[...])).astype(BF16)
    embed_ref[...] = embed
    rows_ref[...] = dot(pick_ref[...], embed).astype(BF16)


def local_kernel(negatives_ref, positives_ref, anchors_ref, embed_ref, out_ref, live_ref, spread_ref, grad_ref, *, scale):
    embed = embed_ref[...]
    out_ref[...] = embed
    nodes = embed.shape[0]
    peers = negatives_ref.shape[0]
    slots = jnp.concatenate([negatives_ref[j] for j in range(peers)], axis=1)
    live_ref[...] = column_counts(slots.T, nodes)
    anchors = jnp.concatenate([anchors_ref[j : j + 1, :] for j in range(peers)], axis=1)
    spread_ref[...] = row_counts(anchors, nodes).astype(BF16)
    first = row_counts(positives_ref[0:1, :], nodes).astype(BF16)
    second = row_counts(positives_ref[1:2, :], nodes).astype(BF16)
    pairs = dot_nt(first, second) + dot_nt(second, first)
    weight = (jax.nn.sigmoid(dot_nt(embed, embed) * scale) - 1.0) * pairs
    grad_ref[...] = dot(weight.astype(BF16), embed)


def score_kernel(got_ref, embed_ref, live_ref, weight_ref, back_ref, *, scale):
    embed = embed_ref[...]
    weight = jax.nn.sigmoid(dot_nt(got_ref[...], embed) * scale) * live_ref[...].astype(F32)
    weight = weight.astype(BF16)
    weight_ref[...] = weight
    back_ref[...] = dot(weight, embed).astype(BF16)


def final_kernel(spread_ref, terms_ref, weight_ref, got_ref, grad_ref, out_ref):
    total = grad_ref[...] + dot_tn(weight_ref[...], got_ref[...]) + dot(spread_ref[...], terms_ref[...])
    out_ref[...] = total.astype(BF16)


def passed_along(block, axis, distance):
    devices = range(lax.axis_size(axis))
    route = [(i - distance, i) for i in devices if i - distance in devices]
    return lax.ppermute(block, axis, route)


def exchanged(rows, peers):
    block = rows.reshape(peers, -1, rows.shape[1])
    return lax.all_to_all(block, "wide", split_axis=0, concat_axis=0, tiled=True).reshape(rows.shape)


def body(features, w_self, w_neigh, boundary, neighbors, anchors, negatives, positives):
    nodes, width = features.shape
    scale = 1.0 / math.sqrt(width)
    peers, anch = anchors.shape
    slots = peers * anch
    edge = boundary.shape[2]
    given = (boundary, anchors, features, neighbors.T)
    _, anchors, features, neighbors, pick, up, down = call(
        head_kernel,
        [shape(x.shape, x.dtype) for x in given] + [shape((slots, nodes), BF16)] + [shape((edge, width), BF16)] * 2,
        *given,
        from_hbm=len(given),
        scratch=[pltpu.SemaphoreType.DMA((len(given),))],
    )
    below = passed_along(up, "dom", 1)
    above = passed_along(down, "dom", -1)
    own, summed, counts, degree = call(
        own_kernel,
        [
            shape((nodes, width), F32),
            shape((nodes, width), F32),
            shape((nodes, 2 * edge), BF16),
            shape((nodes, 1), F32),
        ],
        w_self,
        features,
        neighbors,
        from_hbm=1,
        scratch=[pltpu.VMEM(w_self.shape, BF16), pltpu.SemaphoreType.DMA((1,))],
    )
    embed, rows = call(
        embed_kernel,
        [shape((nodes, width), BF16), shape((slots, width), BF16)],
        below,
        above,
        counts,
        degree,
        summed,
        own,
        w_neigh,
        pick,
    )
    got = exchanged(rows, peers)
    embedded, live, spread, grad = call(
        local_kernel,
        [jax.ShapeDtypeStruct((nodes, width), BF16), shape((slots, nodes), BF16), shape((nodes, slots), BF16), shape((nodes, width), F32)],
        negatives.transpose(0, 2, 1),
        positives.T,
        anchors,
        embed,
        scale=scale,
    )
    weight, back = call(
        score_kernel,
        [shape((slots, nodes), BF16), shape((slots, width), BF16)],
        got,
        embed,
        live,
        scale=scale,
    )
    terms = exchanged(back, peers)
    [out] = call(final_kernel, [jax.ShapeDtypeStruct((nodes, width), BF16)], spread, terms, weight, got, grad)
    return (embedded, out)


def solution(mesh):
    split = P(("dom", "wide"))
    return jax.shard_map(
        body,
        mesh=mesh,
        in_specs=(split, P(), P(), split, split, split, split, split),
        out_specs=(split, split),
        check_vma=False,
    )
```

```python
import functools
import math

import jax
import jax.numpy as jnp
from jax import lax
from jax.experimental import pallas as pl
from jax.experimental.pallas import tpu as pltpu
from jax.sharding import PartitionSpec as P

F32 = jnp.float32
BF16 = jnp.bfloat16


def shape(dims, dtype):
    return pltpu.VMEM(dims, dtype)


def call(kernel, outs, *operands, from_hbm=0, scratch=(), aliases=None, **static):
    spaces = [pltpu.HBM] * from_hbm + [pltpu.VMEM] * (len(operands) - from_hbm)
    out_spaces = [pltpu.HBM if isinstance(x, jax.ShapeDtypeStruct) else pltpu.VMEM for x in outs]
    return pl.pallas_call(
        functools.partial(kernel, **static) if static else kernel,
        out_shape=outs,
        in_specs=[pl.BlockSpec(memory_space=space) for space in spaces],
        out_specs=[pl.BlockSpec(memory_space=space) for space in out_spaces],
        scratch_shapes=list(scratch),
        input_output_aliases=aliases or {},
        compiler_params=pltpu.CompilerParams(vmem_limit_bytes=4 * 2**20),
        name=kernel.__name__,
    )(*[pltpu.with_memory_space_constraint(x, space) for x, space in zip(operands, spaces)])


def fetch(pairs, arrived):
    copies = [pltpu.make_async_copy(a, b, arrived.at[n]) for n, (a, b) in enumerate(pairs)]
    for copy in copies:
        copy.start()
    return copies


def dot(a, b):
    return jnp.dot(a, b, preferred_element_type=F32)


def dot_nt(a, b):
    return lax.dot_general(a, b, (((1,), (1,)), ((), ())), preferred_element_type=F32)


def dot_tn(a, b):
    return lax.dot_general(a, b, (((0,), (0,)), ((), ())), preferred_element_type=F32)


def column_counts(columns, width):
    rows, slots = columns.shape
    lanes = (lax.broadcasted_iota(jnp.int32, (rows, width), 1) - 128).astype(BF16)
    columns = (columns - 128).astype(BF16)
    total = jnp.zeros((rows, width), BF16)
    one, zero = jnp.ones((), BF16), jnp.zeros((), BF16)
    for slot in range(slots):
        total = total + jnp.where(columns[:, slot : slot + 1] == lanes, one, zero)
    return total


def row_counts(rows, height):
    slots, width = rows.shape
    levels = lax.broadcasted_iota(jnp.int32, (height, width), 0)
    total = jnp.zeros((height, width), F32)
    for slot in range(slots):
        total = total + jnp.where(rows[slot : slot + 1, :] == levels, 1.0, 0.0)
    return total


def head_kernel(*refs):
    fetched = 5
    held, (pick_ref, up_ref, down_ref, arrived) = refs[fetched : 2 * fetched], refs[2 * fetched :]
    copies = fetch(zip(refs[:fetched], held), arrived)
    lists_ref, anchors_ref, features_ref = held[:3]
    nodes = features_ref.shape[0]
    copies[0].wait()
    onehots = [row_counts(lists_ref[0, side : side + 1, :], nodes).astype(BF16) for side in range(2)]
    copies[1].wait()
    slots = jnp.concatenate([anchors_ref[j : j + 1, :] for j in range(anchors_ref.shape[0])], axis=1)
    pick_ref[...] = column_counts(slots.T, nodes)
    copies[2].wait()
    for onehot, out in zip(onehots, (up_ref, down_ref)):
        out[...] = dot_tn(onehot, features_ref[...]).astype(BF16)
    for copy in copies[3:]:
        copy.wait()


def own_kernel(*refs, turn, made):
    w_self_hbm, features_ref, neighbors_ref, negatives_ref, positives_ref, anchors_ref = refs[:6]
    own_ref, summed_ref, counts_ref, degree_ref, live_ref, spread_ref, pairs_ref = refs[len(refs) - made - 2 : -2]
    w_self_ref, arrived = refs[-2:]

    @pl.when(waits_long() if turn == 0 else jnp.logical_not(waits_long()))
    def _():
        [copy] = fetch(((w_self_hbm, w_self_ref),), arrived)
        features = features_ref[...]
        nodes = features.shape[0]
        edge = counts_ref.shape[1]
        peers = negatives_ref.shape[0]
        counts = column_counts(neighbors_ref[...].T, nodes + edge)
        degree_ref[...] = jnp.sum(counts.astype(F32), axis=1, keepdims=True)
        counts_ref[...] = counts[:, nodes:]
        summed_ref[...] = dot(counts[:, :nodes], features)
        slots = jnp.concatenate([negatives_ref[j] for j in range(peers)], axis=1)
        live_ref[...] = column_counts(slots.T, nodes)
        anchors = jnp.concatenate([anchors_ref[j : j + 1, :] for j in range(peers)], axis=1)
        spread_ref[...] = row_counts(anchors, nodes).astype(BF16)
        first = row_counts(positives_ref[0:1, :], nodes).astype(BF16)
        second = row_counts(positives_ref[1:2, :], nodes).astype(BF16)
        pairs_ref[...] = dot_nt(first, second) + dot_nt(second, first)
        copy.wait()
        own_ref[...] = dot(features, w_self_ref[...])


def embed_kernel(below_ref, above_ref, counts_ref, degree_ref, summed_ref, own_ref, w_neigh_ref, pick_ref, embed_ref, rows_ref):
    rows = below_ref.shape[0]
    summed = summed_ref[...] + dot(counts_ref[:, :rows], below_ref[...]) + dot(counts_ref[:, rows:], above_ref[...])
    mean = (summed / degree_ref[...]).astype(BF16)
    embed = (own_ref[...] + dot(mean, w_neigh_ref[...])).astype(BF16)
    embed_ref[...] = embed
    rows_ref[...] = dot(pick_ref[...], embed).astype(BF16)


def score_kernel(got_ref, embed_ref, live_ref, pairs_ref, weight_ref, back_ref, grad_ref, out_ref, sent, *, scale):
    copy = pltpu.make_async_copy(embed_ref, out_ref, sent.at[0])
    copy.start()
    embed = embed_ref[...]
    weight = jax.nn.sigmoid(dot_nt(got_ref[...], embed) * scale) * live_ref[...].astype(F32)
    weight = weight.astype(BF16)
    weight_ref[...] = weight
    back_ref[...] = dot(weight, embed).astype(BF16)
    weight = (jax.nn.sigmoid(dot_nt(embed, embed) * scale) - 1.0) * pairs_ref[...]
    grad_ref[...] = dot(weight.astype(BF16), embed)
    copy.wait()


def final_kernel(spread_ref, terms_ref, weight_ref, got_ref, grad_ref, out_ref):
    total = grad_ref[...] + dot_tn(weight_ref[...], got_ref[...]) + dot(spread_ref[...], terms_ref[...])
    out_ref[...] = total.astype(BF16)


ROW = 8


def waits_long():
    return lax.rem(lax.axis_index("dom"), ROW) == 0


def passed_along(block, axis, distance):
    devices = range(lax.axis_size(axis))
    route = [(i - distance, i) for i in devices if i - distance in devices]
    return lax.ppermute(block, axis, route)


def exchanged(rows, peers):
    block = rows.reshape(peers, -1, rows.shape[1])
    return lax.all_to_all(block, "wide", split_axis=0, concat_axis=0, tiled=True).reshape(rows.shape)


def body(features, w_self, w_neigh, boundary, neighbors, anchors, negatives, positives):
    nodes, width = features.shape
    scale = 1.0 / math.sqrt(width)
    peers, anch = anchors.shape
    slots = peers * anch
    edge = boundary.shape[2]
    given = (boundary, anchors, features, neighbors.T, positives.T)
    _, anchors, features, neighbors, positives, pick, up, down = call(
        head_kernel,
        [shape(x.shape, x.dtype) for x in given] + [shape((slots, nodes), BF16)] + [shape((edge, width), BF16)] * 2,
        *given,
        from_hbm=len(given),
        scratch=[pltpu.SemaphoreType.DMA((len(given),))],
    )
    local = (w_self, features, neighbors, negatives.transpose(0, 2, 1), positives, anchors)
    made = [
        shape((nodes, width), F32),
        shape((nodes, width), F32),
        shape((nodes, 2 * edge), BF16),
        shape((nodes, 1), F32),
        shape((slots, nodes), BF16),
        shape((nodes, slots), BF16),
        shape((nodes, nodes), F32),
    ]
    below = passed_along(up, "dom", 1)
    room = [pltpu.VMEM(w_self.shape, BF16), pltpu.SemaphoreType.DMA((1,))]
    early = call(own_kernel, made, *local, from_hbm=1, scratch=room, turn=0, made=len(made))
    down, early = lax.optimization_barrier((down, early))
    above = passed_along(down, "dom", -1)
    aliases = {len(local) + n: n for n in range(len(made))}
    own, summed, counts, degree, live, spread, pairs = call(
        own_kernel, made, *local, *early, from_hbm=1, scratch=room, aliases=aliases, turn=1, made=len(made)
    )
    embed, rows = call(
        embed_kernel,
        [shape((nodes, width), BF16), shape((slots, width), BF16)],
        below,
        above,
        counts,
        degree,
        summed,
        own,
        w_neigh,
        pick,
    )
    got = exchanged(rows, peers)
    weight, back, grad, embedded = call(
        score_kernel,
        [
            shape((slots, nodes), BF16),
            shape((slots, width), BF16),
            shape((nodes, width), F32),
            jax.ShapeDtypeStruct((nodes, width), BF16),
        ],
        got,
        embed,
        live,
        pairs,
        scale=scale,
        scratch=[pltpu.SemaphoreType.DMA((1,))],
    )
    terms = exchanged(back, peers)
    [out] = call(final_kernel, [shape((nodes, width), BF16)], spread, terms, weight, got, grad)
    return (embedded, out)


def solution(mesh):
    split = P(("dom", "wide"))
    return jax.shard_map(
        body,
        mesh=mesh,
        in_specs=(split, P(), P(), split, split, split, split, split),
        out_specs=(split, split),
        check_vma=False,
    )
```

```python
import functools
import math

import jax
import jax.numpy as jnp
from jax import lax
from jax.experimental import pallas as pl
from jax.experimental.pallas import tpu as pltpu
from jax.sharding import PartitionSpec as P

F32 = jnp.float32
BF16 = jnp.bfloat16


def shape(dims, dtype):
    return pltpu.VMEM(dims, dtype)


def call(kernel, outs, *operands, from_hbm=0, scratch=(), aliases=None, **static):
    spaces = [pltpu.HBM] * from_hbm + [pltpu.VMEM] * (len(operands) - from_hbm)
    out_spaces = [pltpu.HBM if isinstance(x, jax.ShapeDtypeStruct) else pltpu.VMEM for x in outs]
    return pl.pallas_call(
        functools.partial(kernel, **static) if static else kernel,
        out_shape=outs,
        in_specs=[pl.BlockSpec(memory_space=space) for space in spaces],
        out_specs=[pl.BlockSpec(memory_space=space) for space in out_spaces],
        scratch_shapes=list(scratch),
        input_output_aliases=aliases or {},
        compiler_params=pltpu.CompilerParams(vmem_limit_bytes=4 * 2**20),
        name=kernel.__name__,
    )(*[pltpu.with_memory_space_constraint(x, space) for x, space in zip(operands, spaces)])


def fetch(pairs, arrived):
    copies = [pltpu.make_async_copy(a, b, arrived.at[n]) for n, (a, b) in enumerate(pairs)]
    for copy in copies:
        copy.start()
    return copies


def dot(a, b):
    return jnp.dot(a, b, preferred_element_type=F32)


def dot_nt(a, b):
    return lax.dot_general(a, b, (((1,), (1,)), ((), ())), preferred_element_type=F32)


def dot_tn(a, b):
    return lax.dot_general(a, b, (((0,), (0,)), ((), ())), preferred_element_type=F32)


def column_counts(columns, width):
    rows, slots = columns.shape
    lanes = (lax.broadcasted_iota(jnp.int32, (rows, width), 1) - 128).astype(BF16)
    columns = (columns - 128).astype(BF16)
    total = jnp.zeros((rows, width), BF16)
    one, zero = jnp.ones((), BF16), jnp.zeros((), BF16)
    for slot in range(slots):
        total = total + jnp.where(columns[:, slot : slot + 1] == lanes, one, zero)
    return total


def row_counts(rows, height):
    slots, width = rows.shape
    levels = lax.broadcasted_iota(jnp.int32, (height, width), 0)
    total = jnp.zeros((height, width), F32)
    for slot in range(slots):
        total = total + jnp.where(rows[slot : slot + 1, :] == levels, 1.0, 0.0)
    return total


def head_kernel(lists_hbm, features_hbm, lists_ref, features_ref, up_ref, down_ref, arrived):
    lists_here, features_here = fetch(((lists_hbm, lists_ref), (features_hbm, features_ref)), arrived)
    lists_here.wait()
    nodes = features_ref.shape[0]
    onehots = [row_counts(lists_ref[0, side : side + 1, :], nodes).astype(BF16) for side in range(2)]
    features_here.wait()
    for onehot, out in zip(onehots, (up_ref, down_ref)):
        out[...] = dot_tn(onehot, features_ref[...]).astype(BF16)


def own_kernel(*refs, turn, made):
    given, (features_ref, negatives_ref) = refs[:4], refs[4:6]
    outs, held, arrived = refs[len(refs) - made - 5 : -5], refs[-5:-1], refs[-1]
    own_ref, summed_ref, counts_ref, degree_ref, pick_ref, live_ref, spread_ref, pairs_ref = outs
    neighbors_ref, anchors_ref, positives_ref, w_self_ref = held

    @pl.when(waits_long() if turn == 0 else jnp.logical_not(waits_long()))
    def _():
        copies = fetch(zip(given, held), arrived)
        features = features_ref[...]
        nodes = features.shape[0]
        edge = counts_ref.shape[1]
        peers = negatives_ref.shape[0]
        slots = jnp.concatenate([negatives_ref[j] for j in range(peers)], axis=1)
        live_ref[...] = column_counts(slots.T, nodes)
        copies[0].wait()
        counts = column_counts(neighbors_ref[...].T, nodes + edge)
        degree_ref[...] = jnp.sum(counts.astype(F32), axis=1, keepdims=True)
        counts_ref[...] = counts[:, nodes:]
        summed_ref[...] = dot(counts[:, :nodes], features)
        copies[1].wait()
        anchors = jnp.concatenate([anchors_ref[j : j + 1, :] for j in range(peers)], axis=1)
        pick_ref[...] = column_counts(anchors.T, nodes)
        spread_ref[...] = row_counts(anchors, nodes).astype(BF16)
        copies[2].wait()
        first = row_counts(positives_ref[0:1, :], nodes).astype(BF16)
        second = row_counts(positives_ref[1:2, :], nodes).astype(BF16)
        pairs_ref[...] = dot_nt(first, second) + dot_nt(second, first)
        copies[3].wait()
        own_ref[...] = dot(features, w_self_ref[...])


def embed_kernel(below_ref, above_ref, counts_ref, degree_ref, summed_ref, own_ref, w_neigh_ref, pick_ref, embed_ref, rows_ref):
    rows = below_ref.shape[0]
    summed = summed_ref[...] + dot(counts_ref[:, :rows], below_ref[...]) + dot(counts_ref[:, rows:], above_ref[...])
    mean = (summed / degree_ref[...]).astype(BF16)
    embed = (own_ref[...] + dot(mean, w_neigh_ref[...])).astype(BF16)
    embed_ref[...] = embed
    rows_ref[...] = dot(pick_ref[...], embed).astype(BF16)


def score_kernel(got_ref, embed_ref, live_ref, pairs_ref, weight_ref, back_ref, grad_ref, out_ref, sent, *, scale):
    copy = pltpu.make_async_copy(embed_ref, out_ref, sent.at[0])
    copy.start()
    embed = embed_ref[...]
    weight = jax.nn.sigmoid(dot_nt(got_ref[...], embed) * scale) * live_ref[...].astype(F32)
    weight = weight.astype(BF16)
    weight_ref[...] = weight
    back_ref[...] = dot(weight, embed).astype(BF16)
    weight = (jax.nn.sigmoid(dot_nt(embed, embed) * scale) - 1.0) * pairs_ref[...]
    grad_ref[...] = dot(weight.astype(BF16), embed)
    copy.wait()


def final_kernel(spread_ref, terms_ref, weight_ref, got_ref, grad_ref, out_ref):
    total = grad_ref[...] + dot_tn(weight_ref[...], got_ref[...]) + dot(spread_ref[...], terms_ref[...])
    out_ref[...] = total.astype(BF16)


ROW = 8


def waits_long():
    return lax.rem(lax.axis_index("dom"), ROW) == 0


def passed_along(block, axis, distance):
    devices = range(lax.axis_size(axis))
    route = [(i - distance, i) for i in devices if i - distance in devices]
    return lax.ppermute(block, axis, route)


def exchanged(rows, peers):
    block = rows.reshape(peers, -1, rows.shape[1])
    return lax.all_to_all(block, "wide", split_axis=0, concat_axis=0, tiled=True).reshape(rows.shape)


def body(features, w_self, w_neigh, boundary, neighbors, anchors, negatives, positives):
    nodes, width = features.shape
    scale = 1.0 / math.sqrt(width)
    peers, anch = anchors.shape
    slots = peers * anch
    edge = boundary.shape[2]
    _, features, up, down = call(
        head_kernel,
        [shape(boundary.shape, boundary.dtype), shape((nodes, width), BF16)] + [shape((edge, width), BF16)] * 2,
        boundary,
        features,
        from_hbm=2,
        scratch=[pltpu.SemaphoreType.DMA((2,))],
    )
    given = (neighbors.T, anchors, positives.T, w_self)
    local = given + (features, negatives.transpose(0, 2, 1))
    made = [
        shape((nodes, width), F32),
        shape((nodes, width), F32),
        shape((nodes, 2 * edge), BF16),
        shape((nodes, 1), F32),
        shape((slots, nodes), BF16),
        shape((slots, nodes), BF16),
        shape((nodes, slots), BF16),
        shape((nodes, nodes), F32),
    ]
    below = passed_along(up, "dom", 1)
    room = [pltpu.VMEM(x.shape, x.dtype) for x in given] + [pltpu.SemaphoreType.DMA((len(given),))]
    early = call(own_kernel, made, *local, from_hbm=len(given), scratch=room, turn=0, made=len(made))
    down, early = lax.optimization_barrier((down, early))
    above = passed_along(down, "dom", -1)
    aliases = {len(local) + n: n for n in range(len(made))}
    own, summed, counts, degree, pick, live, spread, pairs = call(
        own_kernel,
        made,
        *local,
        *early,
        from_hbm=len(given),
        scratch=room,
        aliases=aliases,
        turn=1,
        made=len(made),
    )
    embed, rows = call(
        embed_kernel,
        [shape((nodes, width), BF16), shape((slots, width), BF16)],
        below,
        above,
        counts,
        degree,
        summed,
        own,
        w_neigh,
        pick,
    )
    got = exchanged(rows, peers)
    weight, back, grad, embedded = call(
        score_kernel,
        [
            shape((slots, nodes), BF16),
            shape((slots, width), BF16),
            shape((nodes, width), F32),
            jax.ShapeDtypeStruct((nodes, width), BF16),
        ],
        got,
        embed,
        live,
        pairs,
        scale=scale,
        scratch=[pltpu.SemaphoreType.DMA((1,))],
    )
    terms = exchanged(back, peers)
    [out] = call(final_kernel, [shape((nodes, width), BF16)], spread, terms, weight, got, grad)
    return (embedded, out)


def solution(mesh):
    split = P(("dom", "wide"))
    return jax.shard_map(
        body,
        mesh=mesh,
        in_specs=(split, P(), P(), split, split, split, split, split),
        out_specs=(split, split),
        check_vma=False,
    )
```

```python
import functools
import math

import jax
import jax.numpy as jnp
from jax import lax
from jax.experimental import pallas as pl
from jax.experimental.pallas import tpu as pltpu
from jax.sharding import PartitionSpec as P

F32 = jnp.float32
BF16 = jnp.bfloat16


def shape(dims, dtype):
    return pltpu.VMEM(dims, dtype)


def call(kernel, outs, *operands, from_hbm=0, scratch=(), aliases=None, **static):
    spaces = [pltpu.HBM] * from_hbm + [pltpu.VMEM] * (len(operands) - from_hbm)
    out_spaces = [pltpu.HBM if isinstance(x, jax.ShapeDtypeStruct) else pltpu.VMEM for x in outs]
    return pl.pallas_call(
        functools.partial(kernel, **static) if static else kernel,
        out_shape=outs,
        in_specs=[pl.BlockSpec(memory_space=space) for space in spaces],
        out_specs=[pl.BlockSpec(memory_space=space) for space in out_spaces],
        scratch_shapes=list(scratch),
        input_output_aliases=aliases or {},
        compiler_params=pltpu.CompilerParams(vmem_limit_bytes=4 * 2**20),
        name=kernel.__name__,
    )(*[pltpu.with_memory_space_constraint(x, space) for x, space in zip(operands, spaces)])


def fetch(pairs, arrived):
    copies = [pltpu.make_async_copy(a, b, arrived.at[n]) for n, (a, b) in enumerate(pairs)]
    for copy in copies:
        copy.start()
    return copies


def dot(a, b):
    return jnp.dot(a, b, preferred_element_type=F32)


def dot_nt(a, b):
    return lax.dot_general(a, b, (((1,), (1,)), ((), ())), preferred_element_type=F32)


def dot_tn(a, b):
    return lax.dot_general(a, b, (((0,), (0,)), ((), ())), preferred_element_type=F32)


def column_counts(columns, width):
    rows, slots = columns.shape
    lanes = (lax.broadcasted_iota(jnp.int32, (rows, width), 1) - 128).astype(BF16)
    columns = (columns - 128).astype(BF16)
    total = jnp.zeros((rows, width), BF16)
    one, zero = jnp.ones((), BF16), jnp.zeros((), BF16)
    for slot in range(slots):
        total = total + jnp.where(columns[:, slot : slot + 1] == lanes, one, zero)
    return total


def row_counts(rows, height):
    slots, width = rows.shape
    levels = lax.broadcasted_iota(jnp.int32, (height, width), 0)
    total = jnp.zeros((height, width), F32)
    for slot in range(slots):
        total = total + jnp.where(rows[slot : slot + 1, :] == levels, 1.0, 0.0)
    return total


def head_kernel(lists_hbm, features_hbm, lists_ref, features_ref, up_ref, down_ref, arrived):
    lists_here, features_here = fetch(((lists_hbm, lists_ref), (features_hbm, features_ref)), arrived)
    lists_here.wait()
    nodes = features_ref.shape[0]
    onehots = [row_counts(lists_ref[0, side : side + 1, :], nodes).astype(BF16) for side in range(2)]
    features_here.wait()
    for onehot, out in zip(onehots, (up_ref, down_ref)):
        out[...] = dot_tn(onehot, features_ref[...]).astype(BF16)


def own_kernel(*refs, turn, made):
    given, (features_ref, negatives_ref) = refs[:4], refs[4:6]
    outs, held, arrived = refs[len(refs) - made - 5 : -5], refs[-5:-1], refs[-1]
    own_ref, summed_ref, counts_ref, degree_ref, pick_ref, live_ref, spread_ref, pairs_ref = outs
    neighbors_ref, anchors_ref, positives_ref, w_self_ref = held

    @pl.when(waits_long() if turn == 0 else jnp.logical_not(waits_long()))
    def _():
        copies = fetch(zip(given, held), arrived)
        features = features_ref[...]
        nodes = features.shape[0]
        edge = counts_ref.shape[1]
        peers = negatives_ref.shape[0]
        slots = jnp.concatenate([negatives_ref[j] for j in range(peers)], axis=1)
        live_ref[...] = column_counts(slots.T, nodes)
        copies[0].wait()
        counts = column_counts(neighbors_ref[...].T, nodes + edge)
        degree_ref[...] = jnp.sum(counts.astype(F32), axis=1, keepdims=True)
        counts_ref[...] = counts[:, nodes:]
        summed_ref[...] = dot(counts[:, :nodes], features)
        copies[1].wait()
        anchors = jnp.concatenate([anchors_ref[j : j + 1, :] for j in range(peers)], axis=1)
        pick_ref[...] = column_counts(anchors.T, nodes)
        spread_ref[...] = row_counts(anchors, nodes).astype(BF16)
        copies[2].wait()
        first = row_counts(positives_ref[0:1, :], nodes).astype(BF16)
        second = row_counts(positives_ref[1:2, :], nodes).astype(BF16)
        pairs_ref[...] = dot_nt(first, second) + dot_nt(second, first)
        copies[3].wait()
        own_ref[...] = dot(features, w_self_ref[...])


def embed_kernel(below_ref, above_ref, counts_ref, degree_ref, summed_ref, own_ref, w_neigh_ref, pick_ref, embed_ref, rows_ref):
    rows = below_ref.shape[0]
    summed = summed_ref[...] + dot(counts_ref[:, :rows], below_ref[...]) + dot(counts_ref[:, rows:], above_ref[...])
    mean = (summed / degree_ref[...]).astype(BF16)
    embed = (own_ref[...] + dot(mean, w_neigh_ref[...])).astype(BF16)
    embed_ref[...] = embed
    rows_ref[...] = dot(pick_ref[...], embed).astype(BF16)


def score_kernel(got_ref, embed_ref, live_ref, pairs_ref, weight_ref, back_ref, grad_ref, out_ref, sent, *, scale):
    copy = pltpu.make_async_copy(embed_ref, out_ref, sent.at[0])
    copy.start()
    embed = embed_ref[...]
    weight = jax.nn.sigmoid(dot_nt(got_ref[...], embed) * scale) * live_ref[...].astype(F32)
    weight = weight.astype(BF16)
    weight_ref[...] = weight
    back_ref[...] = dot(weight, embed).astype(BF16)
    weight = (jax.nn.sigmoid(dot_nt(embed, embed) * scale) - 1.0) * pairs_ref[...]
    grad_ref[...] = dot(weight.astype(BF16), embed)
    copy.wait()


def final_kernel(spread_ref, terms_ref, weight_ref, got_ref, grad_ref, out_ref, held_ref, sent):
    total = grad_ref[...] + dot_tn(weight_ref[...], got_ref[...]) + dot(spread_ref[...], terms_ref[...])
    held_ref[...] = total.astype(BF16)
    copy = pltpu.make_async_copy(held_ref, out_ref, sent.at[0])
    copy.start()
    copy.wait()


ROW = 8


def waits_long():
    return lax.rem(lax.axis_index("dom"), ROW) == 0


def passed_along(block, axis, distance):
    devices = range(lax.axis_size(axis))
    route = [(i - distance, i) for i in devices if i - distance in devices]
    return lax.ppermute(block, axis, route)


def exchanged(rows, peers):
    block = rows.reshape(peers, -1, rows.shape[1])
    return lax.all_to_all(block, "wide", split_axis=0, concat_axis=0, tiled=True).reshape(rows.shape)


def body(features, w_self, w_neigh, boundary, neighbors, anchors, negatives, positives):
    nodes, width = features.shape
    scale = 1.0 / math.sqrt(width)
    peers, anch = anchors.shape
    slots = peers * anch
    edge = boundary.shape[2]
    _, features, up, down = call(
        head_kernel,
        [shape(boundary.shape, boundary.dtype), shape((nodes, width), BF16)] + [shape((edge, width), BF16)] * 2,
        boundary,
        features,
        from_hbm=2,
        scratch=[pltpu.SemaphoreType.DMA((2,))],
    )
    given = (neighbors.T, anchors, positives.T, w_self)
    local = given + (features, negatives.transpose(0, 2, 1))
    made = [
        shape((nodes, width), F32),
        shape((nodes, width), F32),
        shape((nodes, 2 * edge), BF16),
        shape((nodes, 1), F32),
        shape((slots, nodes), BF16),
        shape((slots, nodes), BF16),
        shape((nodes, slots), BF16),
        shape((nodes, nodes), F32),
    ]
    below = passed_along(up, "dom", 1)
    room = [pltpu.VMEM(x.shape, x.dtype) for x in given] + [pltpu.SemaphoreType.DMA((len(given),))]
    early = call(own_kernel, made, *local, from_hbm=len(given), scratch=room, turn=0, made=len(made))
    down, early = lax.optimization_barrier((down, early))
    above = passed_along(down, "dom", -1)
    aliases = {len(local) + n: n for n in range(len(made))}
    own, summed, counts, degree, pick, live, spread, pairs = call(
        own_kernel,
        made,
        *local,
        *early,
        from_hbm=len(given),
        scratch=room,
        aliases=aliases,
        turn=1,
        made=len(made),
    )
    embed, rows = call(
        embed_kernel,
        [shape((nodes, width), BF16), shape((slots, width), BF16)],
        below,
        above,
        counts,
        degree,
        summed,
        own,
        w_neigh,
        pick,
    )
    got = exchanged(rows, peers)
    weight, back, grad, embedded = call(
        score_kernel,
        [
            shape((slots, nodes), BF16),
            shape((slots, width), BF16),
            shape((nodes, width), F32),
            jax.ShapeDtypeStruct((nodes, width), BF16),
        ],
        got,
        embed,
        live,
        pairs,
        scale=scale,
        scratch=[pltpu.SemaphoreType.DMA((1,))],
    )
    terms = exchanged(back, peers)
    [out] = call(
        final_kernel,
        [jax.ShapeDtypeStruct((nodes, width), BF16)],
        spread,
        terms,
        weight,
        got,
        grad,
        scratch=[pltpu.VMEM((nodes, width), BF16), pltpu.SemaphoreType.DMA((1,))],
    )
    return (embedded, out)


def solution(mesh):
    split = P(("dom", "wide"))
    return jax.shard_map(
        body,
        mesh=mesh,
        in_specs=(split, P(), P(), split, split, split, split, split),
        out_specs=(split, split),
        check_vma=False,
    )
```
